128 devices in a mesh: dx: 8 (over y_lo, x), dy: 8 (over z, core), band: 2 (over y_hi).
Axes of the slice: x: 4, y: 4 (y_hi: 2, y_lo: 2; y = y_hi * 2 + y_lo), z: 4, core: 2. Of those that a mesh axis runs over, the one named last changes fastest.
Arguments:
- orbitals: float32 [8, 8, 3072, 512], P('dx', 'dy', None, 'band'), may hold values from -6 to 6
- hamiltonians: bfloat16 [8, 8, 12, 512, 512], P('dx', 'dy'), as said below
- connectivity: int32 [8, 8, 12, 512], P('dx', 'dy'), may hold values from 0 to 4095, as said below
- face_maps: int32 [8, 8, 4, 256], P('dx', 'dy'), may hold values from 0 to 3071, as said below
Outputs:
- rotated: float32 [8, 8, 3072, 512], P('dx', 'dy', None, 'band')
The draws below stay inside these ranges and needn't reach their ends.
Inputs may be any that keep to these rules, and one draw needn't show every extreme that they name: connectivity[i, j, c, p] is a row of domain (i, j)'s extended node list (3072 owned nodes, then 256 ghost nodes for each of the four faces in the order of the steps); every row of that list is named at least once. face_maps[i, j, k] holds 256 distinct owned nodes. `hamiltonians`: each cell Hamiltonian is symmetric.
All inputs are finite; a program needn't handle non-finite values.
Results may differ from the reference program's by a relative error of at most 0.0038.
The reference program's roundings to bfloat16 on the way (of `faces` and `extended`) count: a program that leaves them out, or rounds other values in their place, can miss the bound.
Values may be sent and summed in bfloat16 or wider, within the bound.
No kernel may reach another device: no remote copies, remote signals or barrier semaphores. Data moves between devices by JAX's collectives and lax.ppermute only.
A program may use at most 128 MiB of HBM per device.

```python
import jax
import jax.numpy as jnp
from jax import lax

NP = 512
ORB = 512
CELLS_DEV = 12
FACE = 256
NS_STEPS = 3
NODES_DEV = 3072
EXT_DEV = 4096
GRID_X = 8
GRID_Y = 8
ALL_NODES = 196608


def draw_hamiltonians(key, part):
    shape = (GRID_X, GRID_Y, CELLS_DEV, NP, NP)
    base = jax.random.normal(key, shape, jnp.float32)
    sym = (base + jnp.swapaxes(base, 3, 4)) / jnp.sqrt(2.0 * NP)
    return sym.astype(jnp.bfloat16)


def draw_connectivity(key, part):
    keys = jax.random.split(jax.random.fold_in(key, 11), GRID_X * GRID_Y)
    slots = CELLS_DEV * NP

    def single(one_key):
        order = jax.random.permutation(one_key, slots)
        return (order % EXT_DEV).astype(jnp.int32)
    table = jax.vmap(single)(keys)
    return table.reshape(GRID_X, GRID_Y, CELLS_DEV, NP)


def draw_face_maps(key, part):
    keys = jax.random.split(jax.random.fold_in(key, 23), GRID_X * GRID_Y * 4)

    def single(one_key):
        return jax.random.permutation(one_key, NODES_DEV)[:FACE].astype(jnp.int32)
    table = jax.vmap(single)(keys)
    return table.reshape(GRID_X, GRID_Y, 4, FACE)


def level_of(rng, shape, cuts, low, high):
    def one(axis_at, parts):
        draws = jax.random.uniform(jax.random.fold_in(jax.random.fold_in(rng, 6), axis_at), (parts,), jnp.float32, low / len(cuts), high / len(cuts))
        return jnp.repeat(jnp.exp(draws), shape[axis_at] // parts).reshape((-1,) + (1,) * (len(shape) - axis_at - 1))

    factor_of = one(*cuts[0])
    for cut in cuts[1:]:
        factor_of = factor_of * one(*cut)
    return factor_of


def noise(key, dims, deviation, most, cuts=(), kind=jnp.bfloat16):
    values = jax.random.normal(key, dims, jnp.float32) * deviation
    if len(cuts) > 0:
        values = level_of(key, dims, cuts, -0.22, 0.18) * values
    return jnp.clip(values, min=-most, max=most).astype(kind)


def setup_inputs(seed: int = 0) -> dict:
    streams_of = jax.random.split(jax.random.key(seed), 5)
    orbitals = noise(streams_of[0], (GRID_X, GRID_Y, NODES_DEV, ORB), 1.0, 6.0, ((0, 8), (1, 8), (3, 2)), jnp.float32)
    hamiltonians = draw_hamiltonians(jax.random.fold_in(streams_of[4], 71), 0)
    connectivity = draw_connectivity(jax.random.fold_in(streams_of[4], 71), 0)
    face_maps = draw_face_maps(jax.random.fold_in(streams_of[4], 71), 0)
    return {"orbitals": orbitals, "hamiltonians": hamiltonians, "connectivity": connectivity, "face_maps": face_maps}


def apply_operator(field, hamiltonians, connectivity, face_maps):
    cols = field.shape[3]
    nodes = field.shape[2]
    faces = jax.vmap(jax.vmap(lambda y, f: jnp.take(y, f.reshape(-1), axis=0).reshape(4, FACE, cols)))(field, face_maps)
    faces = faces.astype(jnp.bfloat16)
    ghosts = [jnp.roll(faces[:, :, 0], 1, 0), jnp.roll(faces[:, :, 1], -1, 0), jnp.roll(faces[:, :, 2], 1, 1), jnp.roll(faces[:, :, 3], -1, 1)]
    extended = jnp.concatenate([field.astype(jnp.bfloat16)] + ghosts, axis=2)
    ext_rows = extended.shape[2]
    domains = GRID_X * GRID_Y

    def domain_work(items):
        ext_block, ham_block, conn_block = items
        index = conn_block.reshape(-1)
        cells = jnp.take(ext_block, index, axis=0).reshape(CELLS_DEV, NP, cols)
        prods = jnp.einsum('cpq,cqo->cpo', ham_block.astype(jnp.float32), cells.astype(jnp.float32))
        return jnp.zeros((ext_rows, cols), jnp.float32).at[index].add(prods.reshape(-1, cols))
    assembled = lax.map(domain_work, (extended.reshape(domains, ext_rows, cols), hamiltonians.reshape(domains, CELLS_DEV, NP, NP), connectivity.reshape(domains, CELLS_DEV, NP)))
    assembled = assembled.reshape(GRID_X, GRID_Y, ext_rows, cols)
    owned_part = assembled[:, :, :nodes]
    ghost_part = assembled[:, :, nodes:].reshape(GRID_X, GRID_Y, 4, FACE, cols)
    backs = jnp.stack([jnp.roll(ghost_part[:, :, 0], -1, 0), jnp.roll(ghost_part[:, :, 1], 1, 0), jnp.roll(ghost_part[:, :, 2], -1, 1), jnp.roll(ghost_part[:, :, 3], 1, 1)], axis=2)
    return jax.vmap(jax.vmap(lambda a, f, b: a.at[f.reshape(-1)].add(b.reshape(-1, cols))))(owned_part, face_maps, backs)

def ortho_factor(gram):
    scale = jnp.sqrt(jnp.sum(gram * gram))
    matrix = gram / scale
    ident = jnp.eye(gram.shape[0], dtype=gram.dtype)
    factor = ident
    for number in range(NS_STEPS):
        middle = 1.5 * ident - 0.5 * jnp.dot(factor, matrix, precision=lax.Precision.HIGHEST)
        matrix = jnp.dot(matrix, middle, precision=lax.Precision.HIGHEST)
        factor = jnp.dot(middle, factor, precision=lax.Precision.HIGHEST)
    return factor / jnp.sqrt(scale)

def reference(orbitals, hamiltonians, connectivity, face_maps):

    def scaled(field):
        return (apply_operator(field, hamiltonians, connectivity, face_maps) - 0.5 * field) / 2.0
    previous = orbitals
    latest = scaled(orbitals)
    for number in range(3):
        following = 2.0 * scaled(latest) - previous
        previous, latest = (latest, following)
    flat = latest.reshape(-1, latest.shape[3])
    gram = jnp.dot(flat.T, flat, precision=lax.Precision.HIGHEST) / ALL_NODES
    factor = ortho_factor(gram)
    rotated = jnp.dot(flat, factor, precision=lax.Precision.HIGHEST)
    return rotated.reshape(latest.shape)
```

```python
import jax
import jax.numpy as jnp
from jax import lax
from jax.experimental import pallas as pl
from jax.experimental.pallas import tpu as pltpu
from jax.sharding import PartitionSpec as P

NS_STEPS = 3
LANES = 128
UNROLL = 16


VMEM = pl.BlockSpec(memory_space=pltpu.VMEM)
SMEM = pl.BlockSpec(memory_space=pltpu.SMEM)


def limit(mib):
    return pltpu.CompilerParams(vmem_limit_bytes=mib << 20)


def pair(start):
    return pl.ds(pl.multiple_of(start, 2), 2)


def gather_rows(index, base, source, target, count):
    def step(number, carry):
        first = number * UNROLL
        for lane in range(UNROLL):
            row = index[base + first + lane]
            target[pair(2 * first + 2 * lane), :] = source[pair(row), :]
        return carry

    lax.fori_loop(0, count // UNROLL, step, 0)


def index_kernel(connection, first, last):
    slots = connection.shape[0]

    def step(number, carry):
        base = number * UNROLL
        for lane in range(UNROLL):
            slot = base + lane
            last[connection[slot]] = 2 * slot
        for lane in range(UNROLL):
            slot = slots - 1 - base - lane
            first[connection[slot]] = 2 * slot
        return carry

    lax.fori_loop(0, slots // UNROLL, step, 0)


def start_kernel(faces, field, current, face_vals, held):
    nodes = field.shape[0]
    chunk = 256

    def step(number, carry):
        block = field[pl.ds(pl.multiple_of(number * chunk, chunk), chunk), :]
        begin = number * 2 * chunk
        current[pl.ds(begin, chunk, stride=2), :] = block[:, :LANES]
        current[pl.ds(begin + 1, chunk, stride=2), :] = block[:, LANES:]
        return carry

    lax.fori_loop(0, nodes // chunk, step, 0)
    gather_rows(faces, 0, current, held, faces.shape[0])
    face_vals[...] = held[...].astype(jnp.bfloat16)


def cells_kernel(scales, connection, first, last, second, extra, current, before, west, east, south, north,
                 hamiltonian, partial, ghosts, extended, cell_in, products):
    owned = current.shape[0]
    face = west.shape[0]
    cells, points, _ = hamiltonian.shape
    alpha, beta, gamma = scales
    extended[:owned, :] = current[...]
    for number, block in enumerate((west, east, south, north)):
        extended[pl.ds(owned + number * face, face), :] = block[...].astype(jnp.float32)
    products[pl.ds(2 * cells * points, 8), :] = jnp.zeros((8, LANES), jnp.float32)

    def cell(number, carry):
        gather_rows(connection, number * points, extended, cell_in, points)
        left = cell_in[pl.ds(0, points, stride=2), :].astype(jnp.bfloat16)
        right = cell_in[pl.ds(1, points, stride=2), :].astype(jnp.bfloat16)
        product = jnp.dot(
            hamiltonian[number],
            jnp.concatenate([left, right], axis=1),
            preferred_element_type=jnp.float32,
        )
        begin = number * 2 * points
        products[pl.ds(begin, points, stride=2), :] = product[:, :LANES]
        products[pl.ds(begin + 1, points, stride=2), :] = product[:, LANES:]
        return carry

    lax.fori_loop(0, cells, cell, 0)

    def combine(number, carry):
        base = number * UNROLL
        for lane in range(UNROLL):
            one = first[base + lane]
            two = second[base + lane]
            extended[pair(2 * base + 2 * lane), :] = products[pair(one), :] + products[pair(two), :]
        return carry

    lax.fori_loop(0, first.shape[0] // UNROLL, combine, 0)

    @pl.when(extra[0] != 0)
    def _():
        def add(slot, carry):
            row = connection[slot]
            half = row // 2
            inner = jnp.logical_and(first[half] != 2 * slot, last[half] != 2 * slot)

            @pl.when(inner)
            def _():
                extended[pair(row), :] = extended[pair(row), :] + products[pair(2 * slot), :]

            return carry

        lax.fori_loop(0, connection.shape[0], add, 0)

    chunk = 512

    def finish(number, carry):
        rows = pl.ds(pl.multiple_of(number * chunk, chunk), chunk)
        value = alpha * extended[rows, :] - beta * current[rows, :]
        if gamma:
            value = value - gamma * before[rows, :]
        partial[rows, :] = value
        return carry

    lax.fori_loop(0, owned // chunk, finish, 0)
    ghosts[...] = alpha * extended[owned:, :]


def add_returned(faces, returned, target):
    count = faces.shape[0] // len(returned)
    for number, block in enumerate(returned):

        def step(turn, carry):
            base = turn * UNROLL
            rows = [faces[number * count + base + lane] for lane in range(UNROLL)]
            sums = [
                target[pair(rows[lane]), :] + block[pair(2 * base + 2 * lane), :] for lane in range(UNROLL)
            ]
            for lane in range(UNROLL):
                target[pair(rows[lane]), :] = sums[lane]
            return carry

        lax.fori_loop(0, count // UNROLL, step, 0)


def faces_kernel(faces, partial, west, east, south, north, current, face_vals, held):
    current[...] = partial[...]
    add_returned(faces, (west, east, south, north), current)
    gather_rows(faces, 0, current, held, faces.shape[0])
    face_vals[...] = held[...].astype(jnp.bfloat16)


def last_kernel(faces, partial, west, east, south, north, exact, rounded, work):
    work[...] = partial[...]
    add_returned(faces, (west, east, south, north), work)
    nodes = exact.shape[0]
    chunk = 256

    def step(number, carry):
        rows = pl.ds(pl.multiple_of(number * chunk, chunk), chunk)
        begin = number * 2 * chunk
        block = jnp.concatenate(
            [work[pl.ds(begin, chunk, stride=2), :], work[pl.ds(begin + 1, chunk, stride=2), :]], axis=1
        )
        exact[rows, :] = block
        rounded[rows, :] = block.astype(jnp.bfloat16)
        return carry

    lax.fori_loop(0, nodes // chunk, step, 0)


def halves(value):
    high = value.astype(jnp.bfloat16)
    return high, (value - high.astype(jnp.float32)).astype(jnp.bfloat16)


def product3(left, right):
    def dot(a, b):
        return jnp.dot(a, b, preferred_element_type=jnp.float32)

    (lh, ll), (rh, rl) = halves(left), halves(right)
    return dot(lh, rh) + (dot(lh, rl) + dot(ll, rh))


def factor_kernel(gram, factor):
    value = gram[...]
    scale = jnp.sqrt(jnp.sum(value * value))
    matrix = value / scale
    size = value.shape[0]
    row = lax.broadcasted_iota(jnp.int32, (size, size), 0)
    column = lax.broadcasted_iota(jnp.int32, (size, size), 1)
    ident = jnp.where(row == column, 1.0, 0.0).astype(jnp.float32)
    current = 1.5 * ident - 0.5 * matrix
    matrix = product3(matrix, current)
    for number in range(1, NS_STEPS):
        middle = 1.5 * ident - 0.5 * product3(current, matrix)
        if number < NS_STEPS - 1:
            matrix = product3(matrix, middle)
        current = product3(middle, current)
    factor[...] = current / jnp.sqrt(scale)


def call(kernel, out, specs, scratch=(), mib=8, out_specs=None, cost=None, **more):
    return pl.pallas_call(
        kernel,
        out_shape=out,
        in_specs=specs,
        out_specs=out_specs if out_specs is not None else jax.tree.map(lambda _: VMEM, out),
        scratch_shapes=scratch,
        compiler_params=limit(mib),
        cost_estimate=cost,
        **more,
    )


def shape(rows, columns, dtype=jnp.float32):
    return jax.ShapeDtypeStruct((rows, columns), dtype)


def passed_along(value, axis, steps):
    count = lax.axis_size(axis)
    pairs = [(source, (source + steps) % count) for source in range(count)]
    return lax.ppermute(value, axis, pairs)


def sent_faces(values):
    values = values.reshape(4, -1, LANES)
    return (
        passed_along(values[0], "dx", 1),
        passed_along(values[1], "dx", -1),
        passed_along(values[2], "dy", 1),
        passed_along(values[3], "dy", -1),
    )


def sent_ghosts(values):
    values = values.reshape(4, -1, LANES)
    return (
        passed_along(values[0], "dx", -1),
        passed_along(values[1], "dx", 1),
        passed_along(values[2], "dy", -1),
        passed_along(values[3], "dy", 1),
    )


def local(orbitals, hamiltonians, connectivity, face_maps):
    field = orbitals[0, 0]
    hamiltonian = hamiltonians[0, 0]
    connection = connectivity[0, 0].reshape(-1)
    faces = 2 * face_maps[0, 0].reshape(-1)
    nodes, columns = field.shape
    wide = columns // LANES
    slots = connection.shape[0]
    face_rows = faces.shape[0]
    rows = nodes + face_rows
    cells, points, _ = hamiltonian.shape

    current, face_vals = call(
        start_kernel,
        [shape(wide * nodes, LANES), shape(wide * face_rows, LANES, jnp.bfloat16)],
        [SMEM, VMEM],
        [pltpu.VMEM((wide * face_rows, LANES), jnp.float32)],
    )(faces, field)
    received = sent_faces(face_vals)

    table = jax.ShapeDtypeStruct((rows,), jnp.int32)
    first, last = call(
        index_kernel, [table, table], [SMEM], out_specs=[SMEM, SMEM],
        cost=pl.CostEstimate(flops=10**9, bytes_accessed=10**7, transcendentals=0),
    )(connection)
    single = first == last
    second = jnp.where(single, 2 * slots, last)
    covered = jnp.sum(jnp.where(single, 1, 2))
    extra = jnp.where(covered != slots, 1, 0).astype(jnp.int32).reshape(1)
    doubled = 2 * connection

    previous = current
    for number in range(4):
        scales = (0.5, 0.25, 0.0) if number == 0 else (1.0, 0.5, 1.0)

        def kernel(*refs, scales=scales):
            cells_kernel(scales, *refs)

        partial, ghosts = call(
            kernel,
            [shape(wide * nodes, LANES), shape(wide * face_rows, LANES)],
            [SMEM] * 5 + [VMEM] * 7,
            [
                pltpu.VMEM((wide * rows, LANES), jnp.float32),
                pltpu.VMEM((wide * points, LANES), jnp.float32),
                pltpu.VMEM((wide * slots + 8, LANES), jnp.float32),
            ],
            mib=24,
        )(doubled, first, last, second, extra, current, previous, *received, hamiltonian)
        back = sent_ghosts(ghosts)
        if number < 3:
            previous = current
            current, face_vals = call(
                faces_kernel,
                [shape(wide * nodes, LANES), shape(wide * face_rows, LANES, jnp.bfloat16)],
                [SMEM] + [VMEM] * 5,
                [pltpu.VMEM((wide * face_rows, LANES), jnp.float32)],
                input_output_aliases={1: 0},
            )(faces, partial, *back)
            received = sent_faces(face_vals)
        else:
            exact, rounded = call(
                last_kernel,
                [shape(nodes, columns), shape(nodes, columns, jnp.bfloat16)],
                [SMEM] + [VMEM] * 5,
                [pltpu.VMEM((wide * nodes, LANES), jnp.float32)],
            )(faces, partial, *back)
    return finish(exact, rounded, nodes)


def dot_nodes(left, right):
    return lax.dot_general(left, right, (((0,), (0,)), ((), ())), preferred_element_type=jnp.float32)


def summed(value, axes):
    count = lax.axis_size(axes)
    pieces = value.astype(jnp.bfloat16).reshape(count, -1)
    pieces = lax.all_to_all(pieces, axes, 0, 0, tiled=True)
    piece = jnp.sum(pieces.astype(jnp.float32), axis=0, keepdims=True)
    sums = lax.all_to_all(jnp.broadcast_to(piece, pieces.shape), axes, 0, 0, tiled=True)
    return sums.reshape(value.shape)


def finish(exact, rounded, nodes):
    band = lax.axis_index("band")
    half = nodes // 2
    columns = exact.shape[1]
    total = nodes * lax.axis_size("dx") * lax.axis_size("dy")
    mine = lax.dynamic_slice_in_dim(rounded, band * half, half, 0)
    theirs = lax.dynamic_slice_in_dim(rounded, (1 - band) * half, half, 0)
    other_mine = passed_along(theirs, "band", 1)
    other_theirs = passed_along(mine, "band", 1)
    whole = dot_nodes(rounded, rounded)
    cross = dot_nodes(jnp.where(band == 0, mine, other_mine), jnp.where(band == 0, other_mine, mine))
    zero = jnp.zeros_like(whole)
    block = jnp.concatenate(
        [jnp.where(band == 0, whole, zero), jnp.where(band == 0, zero, whole), cross], axis=0
    )
    block = summed(block, ("dx", "dy", "band")) / total
    one, two, three = block[:columns], block[columns:2 * columns], block[2 * columns:]
    gram = jnp.concatenate(
        [jnp.concatenate([one, three], axis=1), jnp.concatenate([three.T, two], axis=1)], axis=0
    )
    factor = call(factor_kernel, shape(2 * columns, 2 * columns), [VMEM], mib=16)(gram)
    own = lax.dynamic_slice(factor, (band * columns, band * columns), (columns, columns))
    across = lax.dynamic_slice(factor, ((1 - band) * columns, band * columns), (columns, columns))
    other = jnp.where(band == 0, jnp.concatenate([other_mine, other_theirs]), jnp.concatenate([other_theirs, other_mine]))
    rotated = jnp.dot(exact, own, precision=lax.Precision.HIGHEST) + jnp.dot(
        other, across.astype(jnp.bfloat16), preferred_element_type=jnp.float32
    )
    return rotated[None, None]


def solution(mesh):
    in_specs = (
        P("dx", "dy", None, "band"),
        P("dx", "dy", None, None, None),
        P("dx", "dy", None, None),
        P("dx", "dy", None, None),
    )
    out_specs = P("dx", "dy", None, "band")
    return jax.shard_map(local, mesh=mesh, in_specs=in_specs, out_specs=out_specs, check_vma=False)
```

```python
import jax
import jax.numpy as jnp
from jax import lax
from jax.experimental import pallas as pl
from jax.experimental.pallas import tpu as pltpu
from jax.sharding import PartitionSpec as P

NS_STEPS = 3
LANES = 128
UNROLL = 64
DISTINCT = 32


VMEM = pl.BlockSpec(memory_space=pltpu.VMEM)
SMEM = pl.BlockSpec(memory_space=pltpu.SMEM)


def limit(mib):
    return pltpu.CompilerParams(vmem_limit_bytes=mib << 20)


def pair(start):
    return pl.ds(pl.multiple_of(start, 2), 2)


def gather_rows(index, base, source, target, count):
    def step(number, carry):
        first = number * UNROLL
        for lane in range(UNROLL):
            row = index[base + first + lane]
            target[pair(2 * first + 2 * lane), :] = source[pair(row), :]
        return carry

    lax.fori_loop(0, count // UNROLL, step, 0)


def table_kernel(connection, one, two, extra):
    slots = connection.shape[1]
    high, low = one.shape
    chunk = 512

    def step(number, total):
        begin = pl.multiple_of(number * chunk, chunk)
        row = connection[:, pl.ds(begin, chunk)]
        slot = begin + lax.broadcasted_iota(jnp.int32, (1, chunk), 1)
        tens = (slot >> 7).astype(jnp.float32)
        units = (slot & 127).astype(jnp.float32)

        def weighted(value, size):
            hit = lax.broadcasted_iota(jnp.int32, (size, chunk), 0) == value
            return jnp.concatenate(
                [jnp.where(hit, jnp.broadcast_to(weight, hit.shape), 0.0) for weight in (jnp.ones_like(tens), tens, units)],
                axis=0,
            ).astype(jnp.bfloat16)

        return total + lax.dot_general(
            weighted(row >> 7, high), weighted(row & 127, low), (((1,), (1,)), ((), ())),
            preferred_element_type=jnp.float32,
        )

    total = lax.fori_loop(0, slots // chunk, step, jnp.zeros((3 * high, 3 * low), jnp.float32))

    def block(left, right):
        return total[left * high:(left + 1) * high, right * low:(right + 1) * low]

    count = block(0, 0)

    def whole(value):
        return value.astype(jnp.int32)

    summed_slots = 128 * whole(block(0, 1)) + whole(block(0, 2))
    squares = 16384 * whole(block(1, 1)) + 256 * whole(block(1, 2)) + whole(block(2, 2))
    apart = whole(jnp.sqrt(jnp.maximum(2 * squares - summed_slots * summed_slots, 0).astype(jnp.float32)) + 0.5)
    single = count < 1.5
    one[...] = jnp.where(single, 2 * summed_slots, summed_slots - apart)
    two[...] = jnp.where(single, 2 * slots, summed_slots + apart)
    extra[0] = jnp.where(jnp.max(count) > 2.5, 1, 0).astype(jnp.int32)


def start_kernel(faces, field, current, face_vals, held):
    nodes = field.shape[0]
    chunk = 256

    def step(number, carry):
        block = field[pl.ds(pl.multiple_of(number * chunk, chunk), chunk), :]
        begin = number * 2 * chunk
        current[pl.ds(begin, chunk, stride=2), :] = block[:, :LANES]
        current[pl.ds(begin + 1, chunk, stride=2), :] = block[:, LANES:]
        return carry

    lax.fori_loop(0, nodes // chunk, step, 0)
    gather_rows(faces, 0, current, held, faces.shape[0])
    face_vals[...] = held[...].astype(jnp.bfloat16)


def combine(connection, one, two, extra, products, target, begin, rows):
    @pl.when(extra[0] == 0)
    def _():
        def step(number, carry):
            base = number * UNROLL
            for lane in range(UNROLL):
                left = one[begin + base + lane]
                right = two[begin + base + lane]
                target[pair(2 * base + 2 * lane), :] = products[pair(left), :] + products[pair(right), :]
            return carry

        lax.fori_loop(0, rows // UNROLL, step, 0)

    @pl.when(extra[0] != 0)
    def _():
        def clear(number, carry):
            target[pl.ds(pl.multiple_of(number * 128, 128), 128), :] = jnp.zeros((128, LANES), jnp.float32)
            return carry

        lax.fori_loop(0, 2 * rows // 128, clear, 0)

        def add(slot, carry):
            row = connection[slot] - 2 * begin

            @pl.when(jnp.logical_and(row >= 0, row < 2 * rows))
            def _():
                target[pair(row), :] = target[pair(row), :] + products[pair(2 * slot), :]

            return carry

        lax.fori_loop(0, connection.shape[0], add, 0)


def cells_kernel(alpha, connection, one, two, extra, current, west, east, south, north, hamiltonian,
                 products, ghosts, extended, cell_in):
    owned = current.shape[0]
    face = west.shape[0]
    cells, points, _ = hamiltonian.shape
    chunk = 512

    def fill(number, carry):
        rows = pl.ds(pl.multiple_of(number * chunk, chunk), chunk)
        extended[rows, :] = current[rows, :]
        return carry

    lax.fori_loop(0, owned // chunk, fill, 0)
    for number, block in enumerate((west, east, south, north)):
        extended[pl.ds(owned + number * face, face), :] = block[...].astype(jnp.float32)
    products[pl.ds(2 * cells * points, 8), :] = jnp.zeros((8, LANES), jnp.float32)

    def cell(number, carry):
        gather_rows(connection, number * points, extended, cell_in, points)
        left = cell_in[pl.ds(0, points, stride=2), :].astype(jnp.bfloat16)
        right = cell_in[pl.ds(1, points, stride=2), :].astype(jnp.bfloat16)
        product = jnp.dot(
            hamiltonian[number],
            jnp.concatenate([left, right], axis=1),
            preferred_element_type=jnp.float32,
        )
        begin = number * 2 * points
        products[pl.ds(begin, points, stride=2), :] = product[:, :LANES]
        products[pl.ds(begin + 1, points, stride=2), :] = product[:, LANES:]
        return carry

    lax.fori_loop(0, cells, cell, 0)
    combine(connection, one, two, extra, products, ghosts, owned // 2, 2 * face)
    if alpha != 1.0:
        ghosts[...] = alpha * ghosts[...]


def owned_kernel(scales, connection, one, two, extra, products, current, before, partial):
    alpha, beta, gamma = scales
    owned = partial.shape[0]
    combine(connection, one, two, extra, products, partial, 0, owned // 2)
    chunk = 512

    def finish(number, carry):
        rows = pl.ds(pl.multiple_of(number * chunk, chunk), chunk)
        value = alpha * partial[rows, :] - beta * current[rows, :]
        if gamma:
            value = value - gamma * before[rows, :]
        partial[rows, :] = value
        return carry

    lax.fori_loop(0, owned // chunk, finish, 0)


def add_returned(faces, returned, target):
    count = faces.shape[0] // len(returned)
    for number, block in enumerate(returned):

        def step(turn, carry):
            base = turn * DISTINCT
            rows = [faces[number * count + base + lane] for lane in range(DISTINCT)]
            sums = [
                target[pair(rows[lane]), :] + block[pair(2 * base + 2 * lane), :] for lane in range(DISTINCT)
            ]
            for lane in range(DISTINCT):
                target[pair(rows[lane]), :] = sums[lane]
            return carry

        lax.fori_loop(0, count // DISTINCT, step, 0)


def faces_kernel(faces, partial, west, east, south, north, current, face_vals, held):
    add_returned(faces, (west, east, south, north), current)
    gather_rows(faces, 0, current, held, faces.shape[0])
    face_vals[...] = held[...].astype(jnp.bfloat16)


def last_kernel(band, faces, partial, west, east, south, north, exact, mine, theirs, work):
    add_returned(faces, (west, east, south, north), work)
    half = mine.shape[0]
    chunk = 256

    for start, rounded in ((band[0] * half, mine), ((1 - band[0]) * half, theirs)):

        def step(number, carry):
            inner = pl.multiple_of(number * chunk, chunk)
            outer = pl.multiple_of(start + inner, chunk)
            block = jnp.concatenate(
                [work[pl.ds(2 * outer, chunk, stride=2), :], work[pl.ds(2 * outer + 1, chunk, stride=2), :]],
                axis=1,
            )
            exact[pl.ds(outer, chunk), :] = block
            rounded[pl.ds(inner, chunk), :] = block.astype(jnp.bfloat16)
            return carry

        lax.fori_loop(0, half // chunk, step, 0)


def halves(value):
    high = value.astype(jnp.bfloat16)
    return high, (value - high.astype(jnp.float32)).astype(jnp.bfloat16)


def product3(left, right):
    def dot(a, b):
        return jnp.dot(a, b, preferred_element_type=jnp.float32)

    (lh, ll), (rh, rl) = halves(left), halves(right)
    return dot(lh, rh) + (dot(lh, rl) + dot(ll, rh))


def sum_kernel(scale, pieces, sums):
    total = jnp.sum(pieces[...].astype(jnp.float32), axis=0) * scale
    sums[...] = jnp.broadcast_to(total.astype(jnp.bfloat16)[None], sums.shape)


def rotate_kernel(band, blocks, exact, near, far, rotated, factor, work, sems):
    size = exact.shape[1]

    def square(which, part):
        begin = part * 2 * size
        return jnp.concatenate(
            [blocks[which, begin:begin + size, :], blocks[which, begin + size:begin + 2 * size, :]], axis=1
        ).astype(jnp.float32)

    me = band[0]
    cross = square(me, 1) + square(1 - me, 1).T
    value = jnp.concatenate(
        [
            jnp.concatenate([square(me, 0), cross], axis=1),
            jnp.concatenate([cross.T, square(1 - me, 0)], axis=1),
        ],
        axis=0,
    )
    scale = jnp.sqrt(jnp.sum(value * value))
    matrix = value / scale
    row = lax.broadcasted_iota(jnp.int32, value.shape, 0)
    column = lax.broadcasted_iota(jnp.int32, value.shape, 1)
    ident = jnp.where(row == column, 1.0, 0.0).astype(jnp.float32)
    current = 1.5 * ident - 0.5 * matrix
    matrix = product3(matrix, current)
    for number in range(1, NS_STEPS):
        middle = 1.5 * ident - 0.5 * product3(current, matrix)
        if number < NS_STEPS - 1:
            matrix = product3(matrix, middle)
            current = product3(middle, current)
        else:
            factor[...] = product3(middle, current[:, :size]) / jnp.sqrt(scale)

    half = near.shape[0]
    chunk = 512
    own_high, own_low = halves(factor[:size, :])
    cross_high, cross_low = halves(factor[size:, :])

    def dot(a, b):
        return jnp.dot(a, b, preferred_element_type=jnp.float32)

    def copy(index):
        rows = pl.ds(pl.multiple_of(index * chunk, chunk), chunk)
        return pltpu.make_async_copy(work.at[rows], rotated.at[rows], sems.at[index])

    per = half // chunk
    for part, other in ((me, near), (1 - me, far)):
        for turn in range(per):
            index = part * per + turn
            rows = pl.ds(pl.multiple_of(index * chunk, chunk), chunk)
            high, low = halves(exact[rows, :])
            across = other[turn * chunk:(turn + 1) * chunk, :]
            work[rows, :] = (dot(high, own_high) + dot(across, cross_high)) + (
                dot(high, own_low) + dot(low, own_high) + dot(across, cross_low)
            )
            copy(index).start()
    for index in range(2 * per):
        copy(index).wait()


def call(kernel, out, specs, scratch=(), mib=8, out_specs=None, cost=None, **more):
    return pl.pallas_call(
        kernel,
        out_shape=out,
        in_specs=specs,
        out_specs=out_specs if out_specs is not None else jax.tree.map(lambda _: VMEM, out),
        scratch_shapes=scratch,
        compiler_params=limit(mib),
        cost_estimate=cost,
        **more,
    )


def shape(rows, columns, dtype=jnp.float32):
    return jax.ShapeDtypeStruct((rows, columns), dtype)


def passed_along(value, axis, steps):
    count = lax.axis_size(axis)
    pairs = [(source, (source + steps) % count) for source in range(count)]
    return lax.ppermute(value, axis, pairs)


def sent_faces(values):
    values = values.reshape(4, -1, LANES)
    return (
        passed_along(values[0], "dx", 1),
        passed_along(values[1], "dx", -1),
        passed_along(values[2], "dy", 1),
        passed_along(values[3], "dy", -1),
    )


def sent_ghosts(values):
    values = values.reshape(4, -1, LANES)
    return (
        passed_along(values[0], "dx", -1),
        passed_along(values[1], "dx", 1),
        passed_along(values[2], "dy", -1),
        passed_along(values[3], "dy", 1),
    )


def local(orbitals, hamiltonians, connectivity, face_maps):
    field = orbitals[0, 0]
    hamiltonian = hamiltonians[0, 0]
    connection = connectivity[0, 0].reshape(-1)
    faces = 2 * face_maps[0, 0].reshape(-1)
    nodes, columns = field.shape
    wide = columns // LANES
    slots = connection.shape[0]
    face_rows = faces.shape[0]
    rows = nodes + face_rows
    cells, points, _ = hamiltonian.shape

    current, face_vals = call(
        start_kernel,
        [shape(wide * nodes, LANES), shape(wide * face_rows, LANES, jnp.bfloat16)],
        [SMEM, VMEM],
        [pltpu.VMEM((wide * face_rows, LANES), jnp.float32)],
    )(faces, field)
    received = sent_faces(face_vals)

    table = jax.ShapeDtypeStruct((rows // LANES, LANES), jnp.int32)
    one, two, extra = call(
        table_kernel,
        [table, table, jax.ShapeDtypeStruct((1,), jnp.int32)],
        [VMEM],
        out_specs=[VMEM, VMEM, SMEM],
        cost=pl.CostEstimate(flops=10**9, bytes_accessed=10**6, transcendentals=0),
    )(connection.reshape(1, -1))
    tables = (2 * connection, one.reshape(-1), two.reshape(-1), extra)

    previous = current
    for number in range(4):
        scales = (0.5, 0.25, 0.0) if number == 0 else (1.0, 0.5, 1.0)

        def cells_part(*refs, scales=scales):
            cells_kernel(scales[0], *refs)

        def owned_part(*refs, scales=scales):
            owned_kernel(scales, *refs)

        products, ghosts = call(
            cells_part,
            [shape(wide * slots + 8, LANES), shape(wide * face_rows, LANES)],
            [SMEM] * 4 + [VMEM] * 6,
            [
                pltpu.VMEM((wide * rows, LANES), jnp.float32),
                pltpu.VMEM((wide * points, LANES), jnp.float32),
            ],
            mib=12,
            cost=pl.CostEstimate(flops=2 * 10**9, bytes_accessed=10**7, transcendentals=0),
        )(*tables, current, *received, hamiltonian)
        partial = call(
            owned_part,
            shape(wide * nodes, LANES),
            [SMEM] * 4 + [VMEM] * 3,
            mib=4,
            cost=pl.CostEstimate(flops=10**9, bytes_accessed=10**7, transcendentals=0),
        )(*tables, products, current, previous)
        back = sent_ghosts(ghosts)
        if number < 3:
            previous = current
            current, face_vals = call(
                faces_kernel,
                [shape(wide * nodes, LANES), shape(wide * face_rows, LANES, jnp.bfloat16)],
                [SMEM] + [VMEM] * 5,
                [pltpu.VMEM((wide * face_rows, LANES), jnp.float32)],
                input_output_aliases={1: 0},
            )(faces, partial, *back)
            received = sent_faces(face_vals)
        else:
            band = lax.axis_index("band").astype(jnp.int32).reshape(1)
            half = shape(nodes // 2, columns, jnp.bfloat16)
            exact, mine, theirs, _ = call(
                last_kernel,
                [shape(nodes, columns), half, half, shape(wide * nodes, LANES)],
                [SMEM] * 2 + [VMEM] * 5,
                input_output_aliases={2: 3},
            )(band, faces, partial, *back)
    return finish(band, exact, mine, theirs)[None, None]


def dot_nodes(left, right):
    return lax.dot_general(left, right, (((0,), (0,)), ((), ())), preferred_element_type=jnp.float32)


def finish(band, exact, mine, theirs):
    nodes, columns = exact.shape
    domains = lax.axis_size(("dx", "dy"))
    near = passed_along(theirs, "band", 1)
    whole = dot_nodes(mine, mine) + dot_nodes(theirs, theirs)
    cross = dot_nodes(mine, near)
    far = passed_along(mine, "band", 1)
    pieces = jnp.concatenate(
        [whole[:, :LANES], whole[:, LANES:], cross[:, :LANES], cross[:, LANES:]], axis=0
    ).astype(jnp.bfloat16)
    pieces = pieces.reshape(domains, -1, LANES)
    pieces = lax.all_to_all(pieces, ("dx", "dy"), 0, 0, tiled=True)
    scale = 1.0 / (nodes * domains)

    def kernel(*refs):
        sum_kernel(scale, *refs)

    devices = lax.axis_size(("band", "dx", "dy"))
    sums = call(kernel, jax.ShapeDtypeStruct((devices, *pieces.shape[1:]), jnp.bfloat16), [VMEM], mib=4)(pieces)
    sums = lax.all_to_all(sums, ("band", "dx", "dy"), 0, 0, tiled=True)
    blocks = sums.reshape(2, -1, LANES)
    return call(
        rotate_kernel,
        shape(nodes, columns),
        [SMEM] + [VMEM] * 4,
        [
            pltpu.VMEM((2 * columns, columns), jnp.float32),
            pltpu.VMEM((nodes, columns), jnp.float32),
            pltpu.SemaphoreType.DMA((nodes // 512,)),
        ],
        mib=24,
        out_specs=pl.BlockSpec(memory_space=pl.ANY),
    )(band, blocks, exact, near, far)


def solution(mesh):
    in_specs = (
        P("dx", "dy", None, "band"),
        P("dx", "dy", None, None, None),
        P("dx", "dy", None, None),
        P("dx", "dy", None, None),
    )
    out_specs = P("dx", "dy", None, "band")
    return jax.shard_map(local, mesh=mesh, in_specs=in_specs, out_specs=out_specs, check_vma=False)
```

```python
import jax
import jax.numpy as jnp
from jax import lax
from jax.experimental import pallas as pl
from jax.experimental.pallas import tpu as pltpu
from jax.sharding import PartitionSpec as P

NS_STEPS = 3
LANES = 128
DISTINCT = 32


VMEM = pl.BlockSpec(memory_space=pltpu.VMEM)
SMEM = pl.BlockSpec(memory_space=pltpu.SMEM)
ANY = pl.BlockSpec(memory_space=pl.ANY)
CELLS_MIB = 8


def limit(mib):
    return pltpu.CompilerParams(vmem_limit_bytes=mib << 20)


def pair(start):
    return pl.ds(pl.multiple_of(start, 2), 2)


def gather_rows(index, source, target):
    count = target.shape[0] // 2
    for lane in range(count):
        target[2 * lane:2 * lane + 2, :] = source[pair(at(index, lane)), :]


def gather_lines(index, source, target):
    def step(line, carry):
        part = target.at[pl.ds(pl.multiple_of(line * 2 * LANES, 2 * LANES), 2 * LANES)]
        for lane in range(LANES):
            part[2 * lane:2 * lane + 2, :] = source[pair(index[line, lane]), :]
        return carry

    lax.fori_loop(0, index.shape[0], step, 0)


def at(index, lane):
    return index[lane // LANES, lane % LANES]


def table_kernel(connection, one, two, extra):
    slots = connection.shape[1]
    high, low = one.shape
    chunk = 512

    def step(number, total):
        begin = pl.multiple_of(number * chunk, chunk)
        row = connection[:, pl.ds(begin, chunk)]
        slot = begin + lax.broadcasted_iota(jnp.int32, (1, chunk), 1)
        tens = (slot >> 7).astype(jnp.float32)
        units = (slot & 127).astype(jnp.float32)

        def weighted(value, size):
            hit = lax.broadcasted_iota(jnp.int32, (size, chunk), 0) == value
            return jnp.concatenate(
                [jnp.where(hit, jnp.broadcast_to(weight, hit.shape), 0.0) for weight in (jnp.ones_like(tens), tens, units)],
                axis=0,
            ).astype(jnp.bfloat16)

        return total + lax.dot_general(
            weighted(row >> 7, high), weighted(row & 127, low), (((1,), (1,)), ((), ())),
            preferred_element_type=jnp.float32,
        )

    total = lax.fori_loop(0, slots // chunk, step, jnp.zeros((3 * high, 3 * low), jnp.float32))

    def block(left, right):
        return total[left * high:(left + 1) * high, right * low:(right + 1) * low]

    count = block(0, 0)

    def whole(value):
        return value.astype(jnp.int32)

    summed_slots = 128 * whole(block(0, 1)) + whole(block(0, 2))
    squares = 16384 * whole(block(1, 1)) + 256 * whole(block(1, 2)) + whole(block(2, 2))
    apart = whole(jnp.sqrt(jnp.maximum(2 * squares - summed_slots * summed_slots, 0).astype(jnp.float32)) + 0.5)
    single = count < 1.5
    one[...] = jnp.where(single, 2 * summed_slots, summed_slots - apart)
    two[...] = jnp.where(single, 2 * slots, summed_slots + apart)
    extra[0] = jnp.where(jnp.max(count) > 2.5, 1, 0).astype(jnp.int32)


def start_kernel(faces, field, current, face_vals, held):
    nodes = field.shape[0]
    chunk = 256

    def step(number, carry):
        block = field[pl.ds(pl.multiple_of(number * chunk, chunk), chunk), :]
        begin = number * 2 * chunk
        current[pl.ds(begin, chunk, stride=2), :] = block[:, :LANES]
        current[pl.ds(begin + 1, chunk, stride=2), :] = block[:, LANES:]
        return carry

    lax.fori_loop(0, nodes // chunk, step, 0)
    gather_lines(faces, current, held)
    face_vals[...] = held[...].astype(jnp.bfloat16)


def fetches(table, buffers, sems):
    def fetch(number, buffer):
        return pltpu.make_async_copy(table.at[number], buffers[buffer], sems.at[buffer])

    return fetch


def combine(connection, table, extra, products, target, begin, buffers, sems, scratch, sem, started):
    chunks = table.shape[0]
    rows = target.shape[0] // 2
    size = rows // chunks
    ways = len(buffers)
    fetch = fetches(table, buffers, sems)

    @pl.when(extra[0] == 0)
    def _():
        if not started:
            for way in range(ways):
                fetch(way, way).start()

        def step(turn, carry):
            for way in range(ways):
                number = turn * ways + way
                fetch(number, way).wait()
                part = target.at[pl.ds(pl.multiple_of(number * 2 * size, 2 * size), 2 * size)]
                for lane in range(size):
                    left = at(buffers[way], lane)
                    right = at(buffers[way], size + lane)
                    part[2 * lane:2 * lane + 2, :] = products[pair(left), :] + products[pair(right), :]
                if chunks > ways:
                    fetch(jnp.minimum(number + ways, chunks - 1), way).start()
            return carry

        lax.fori_loop(0, chunks // ways, step, 0)
        if chunks > ways:
            for way in range(ways):
                fetch(0, way).wait()

    @pl.when(extra[0] != 0)
    def _():
        if started:
            for way in range(ways):
                fetch(way, way).wait()
        whole = pltpu.make_async_copy(connection, scratch, sem)
        whole.start()

        def clear(number, carry):
            target[pl.ds(pl.multiple_of(number * 128, 128), 128), :] = jnp.zeros((128, LANES), jnp.float32)
            return carry

        lax.fori_loop(0, 2 * rows // 128, clear, 0)
        whole.wait()
        cells, lines, _ = scratch.shape

        def add(slot, carry):
            row = scratch[slot // (lines * LANES), (slot // LANES) % lines, slot % LANES] - 2 * begin

            @pl.when(jnp.logical_and(row >= 0, row < 2 * rows))
            def _():
                target[pair(row), :] = target[pair(row), :] + products[pair(2 * slot), :]

            return carry

        lax.fori_loop(0, cells * lines * LANES, add, 0)


def cells_kernel(alpha, connection, table, extra, current, west, east, south, north, hamiltonian,
                 products, ghosts, extended, even, odd, i0, i1, i2, i3, t0, t1, t2, t3, scratch, sems):
    owned = current.shape[0]
    face = west.shape[0]
    cells, points, _ = hamiltonian.shape
    chunk = 512
    indices, tables = (i0, i1, i2, i3), (t0, t1, t2, t3)
    ways = len(indices)
    fetch = fetches(connection, indices, sems)
    fetch_table = fetches(table, tables, sems.at[pl.ds(ways, ways)])
    for way in range(ways):
        fetch(way, way).start()
    for way in range(ways):
        fetch_table(way, way).start()

    def fill(number, carry):
        rows = pl.ds(pl.multiple_of(number * chunk, chunk), chunk)
        extended[rows, :] = current[rows, :]
        return carry

    lax.fori_loop(0, owned // chunk, fill, 0)
    for number, block in enumerate((west, east, south, north)):
        extended[pl.ds(owned + number * face, face), :] = block[...].astype(jnp.float32)
    products[pl.ds(2 * cells * points, 8), :] = jnp.zeros((8, LANES), jnp.float32)

    def multiply(number, source):
        left = source[pl.ds(0, points, stride=2), :].astype(jnp.bfloat16)
        right = source[pl.ds(1, points, stride=2), :].astype(jnp.bfloat16)
        product = jnp.dot(
            hamiltonian[number],
            jnp.concatenate([left, right], axis=1),
            preferred_element_type=jnp.float32,
        )
        begin = number * 2 * points
        products[pl.ds(begin, points, stride=2), :] = product[:, :LANES]
        products[pl.ds(begin + 1, points, stride=2), :] = product[:, LANES:]

    fetch(0, 0).wait()
    gather_lines(indices[0], extended, even)
    held = (even, odd)

    def cell(turn, carry):
        for way in range(ways):
            number = turn * ways + way
            after = (way + 1) % ways
            fetch(0, after).wait()
            gather_rows(indices[after], extended, held[after % 2])
            multiply(number, held[way % 2])
            fetch(jnp.minimum(number + ways, cells - 1), way).start()
        return carry

    lax.fori_loop(0, cells // ways, cell, 0)
    for way in range(1, ways):
        fetch(0, way).wait()
    combine(connection, table, extra, products, ghosts, owned // 2, tables, sems.at[pl.ds(ways, ways)],
            scratch, sems.at[2 * ways], True)
    if alpha != 1.0:
        ghosts[...] = alpha * ghosts[...]


def owned_kernel(scales, connection, table, extra, products, current, before, partial,
                 t0, t1, t2, t3, scratch, sems):
    alpha, beta, gamma = scales
    owned = partial.shape[0]
    combine(connection, table, extra, products, partial, 0, (t0, t1, t2, t3), sems, scratch, sems.at[4], False)
    chunk = 512

    def finish(number, carry):
        rows = pl.ds(pl.multiple_of(number * chunk, chunk), chunk)
        value = alpha * partial[rows, :] - beta * current[rows, :]
        if gamma:
            value = value - gamma * before[rows, :]
        partial[rows, :] = value
        return carry

    lax.fori_loop(0, owned // chunk, finish, 0)


def add_returned(faces, returned, target):
    count = returned[0].shape[0] // 2
    for number, block in enumerate(returned):
        for base in range(0, count, DISTINCT):
            lanes = range(base, base + DISTINCT)
            rows = [pair(at(faces, number * count + lane)) for lane in lanes]
            sums = [target[row, :] + block[2 * lane:2 * lane + 2, :] for row, lane in zip(rows, lanes)]
            for row, value in zip(rows, sums):
                target[row, :] = value


def faces_kernel(faces, partial, west, east, south, north, current, face_vals, held):
    add_returned(faces, (west, east, south, north), current)
    gather_lines(faces, current, held)
    face_vals[...] = held[...].astype(jnp.bfloat16)


def last_kernel(faces, partial, west, east, south, north, exact, mine, theirs, work):
    add_returned(faces, (west, east, south, north), work)
    half = mine.shape[0]
    chunk = 256
    band = lax.axis_index("band")

    for start, rounded in ((band * half, mine), ((1 - band) * half, theirs)):

        def step(number, carry):
            inner = pl.multiple_of(number * chunk, chunk)
            outer = pl.multiple_of(start + inner, chunk)
            block = jnp.concatenate(
                [work[pl.ds(2 * outer, chunk, stride=2), :], work[pl.ds(2 * outer + 1, chunk, stride=2), :]],
                axis=1,
            )
            exact[pl.ds(outer, chunk), :] = block
            rounded[pl.ds(inner, chunk), :] = block.astype(jnp.bfloat16)
            return carry

        lax.fori_loop(0, half // chunk, step, 0)


def halves(value):
    high = value.astype(jnp.bfloat16)
    return high, (value - high.astype(jnp.float32)).astype(jnp.bfloat16)


def product3(left, right):
    def dot(a, b):
        return jnp.dot(a, b, preferred_element_type=jnp.float32)

    (lh, ll), (rh, rl) = halves(left), halves(right)
    return dot(lh, rh) + (dot(lh, rl) + dot(ll, rh))


def sum_kernel(scale, pieces, sums):
    total = jnp.sum(pieces[...].astype(jnp.float32), axis=0) * scale
    sums[...] = jnp.broadcast_to(total.astype(jnp.bfloat16)[None], sums.shape)


def rotate_kernel(blocks, exact, near, far, rotated, factor, work, sems):
    size = exact.shape[1]

    def square(which, part):
        begin = part * 2 * size
        return jnp.concatenate(
            [blocks[which, begin:begin + size, :], blocks[which, begin + size:begin + 2 * size, :]], axis=1
        ).astype(jnp.float32)

    me = lax.axis_index("band")
    cross = square(me, 1) + square(1 - me, 1).T
    value = jnp.concatenate(
        [
            jnp.concatenate([square(me, 0), cross], axis=1),
            jnp.concatenate([cross.T, square(1 - me, 0)], axis=1),
        ],
        axis=0,
    )
    scale = jnp.sqrt(jnp.sum(value * value))
    matrix = value / scale
    row = lax.broadcasted_iota(jnp.int32, value.shape, 0)
    column = lax.broadcasted_iota(jnp.int32, value.shape, 1)
    ident = jnp.where(row == column, 1.0, 0.0).astype(jnp.float32)
    current = 1.5 * ident - 0.5 * matrix
    matrix = product3(matrix, current)
    for number in range(1, NS_STEPS):
        middle = 1.5 * ident - 0.5 * product3(current, matrix)
        if number < NS_STEPS - 1:
            matrix = product3(matrix, middle)
            current = product3(middle, current)
        else:
            factor[...] = product3(middle, current[:, :size]) / jnp.sqrt(scale)

    half = near.shape[0]
    chunk = 512
    own_high, own_low = halves(factor[:size, :])
    cross_high, cross_low = halves(factor[size:, :])

    def dot(a, b):
        return jnp.dot(a, b, preferred_element_type=jnp.float32)

    def copy(index):
        rows = pl.ds(pl.multiple_of(index * chunk, chunk), chunk)
        return pltpu.make_async_copy(work.at[rows], rotated.at[rows], sems.at[index])

    per = half // chunk
    for part, other in ((me, near), (1 - me, far)):

        def step(turn, carry):
            index = part * per + turn
            rows = pl.ds(pl.multiple_of(index * chunk, chunk), chunk)
            high, low = halves(exact[rows, :])
            across = other[pl.ds(pl.multiple_of(turn * chunk, chunk), chunk), :]
            work[rows, :] = (dot(high, own_high) + dot(across, cross_high)) + (
                dot(high, own_low) + dot(low, own_high) + dot(across, cross_low)
            )
            copy(index).start()
            return carry

        lax.fori_loop(0, per, step, 0)
    for index in range(2 * per):
        copy(index).wait()


def call(kernel, out, specs, scratch=(), mib=3, out_specs=None, cost=None, **more):
    return pl.pallas_call(
        kernel,
        out_shape=out,
        in_specs=specs,
        out_specs=out_specs if out_specs is not None else jax.tree.map(lambda _: VMEM, out),
        scratch_shapes=scratch,
        compiler_params=limit(mib),
        cost_estimate=cost,
        **more,
    )


def shape(rows, columns, dtype=jnp.float32):
    return jax.ShapeDtypeStruct((rows, columns), dtype)


def passed_along(value, axis, steps):
    count = lax.axis_size(axis)
    pairs = [(source, (source + steps) % count) for source in range(count)]
    return lax.ppermute(value, axis, pairs)


def sent_faces(values):
    values = values.reshape(4, -1, LANES)
    return (
        passed_along(values[0], "dx", 1),
        passed_along(values[1], "dx", -1),
        passed_along(values[2], "dy", 1),
        passed_along(values[3], "dy", -1),
    )


def sent_ghosts(values):
    values = values.reshape(4, -1, LANES)
    return (
        passed_along(values[0], "dx", -1),
        passed_along(values[1], "dx", 1),
        passed_along(values[2], "dy", -1),
        passed_along(values[3], "dy", 1),
    )


def local(orbitals, hamiltonians, connectivity, face_maps):
    field = orbitals[0, 0]
    hamiltonian = hamiltonians[0, 0]
    connection = connectivity[0, 0].reshape(-1)
    faces = 2 * face_maps[0, 0].reshape(-1, LANES)
    nodes, columns = field.shape
    wide = columns // LANES
    slots = connection.shape[0]
    face_rows = faces.size
    rows = nodes + face_rows
    cells, points, _ = hamiltonian.shape

    current, face_vals = call(
        start_kernel,
        [shape(wide * nodes, LANES), shape(wide * face_rows, LANES, jnp.bfloat16)],
        [SMEM, VMEM],
        [pltpu.VMEM((wide * face_rows, LANES), jnp.float32)],
    )(faces, field)
    received = sent_faces(face_vals)

    table = jax.ShapeDtypeStruct((rows // LANES, LANES), jnp.int32)
    one, two, extra = call(
        table_kernel,
        [table, table, jax.ShapeDtypeStruct((1,), jnp.int32)],
        [VMEM],
        out_specs=[VMEM, VMEM, SMEM],
        cost=pl.CostEstimate(flops=10**9, bytes_accessed=10**6, transcendentals=0),
    )(connection.reshape(1, -1))
    doubled = 2 * connection.reshape(cells, -1, LANES)
    pairs = jnp.concatenate([one.reshape(-1, 2, LANES), two.reshape(-1, 2, LANES)], axis=1)
    chunks = nodes // (2 * LANES)
    index = pltpu.SMEM((points // LANES, LANES), jnp.int32)
    table = pltpu.SMEM((4, LANES), jnp.int32)
    scratch = pltpu.SMEM(doubled.shape, jnp.int32)

    previous = current
    for number in range(4):
        scales = (0.5, 0.25, 0.0) if number == 0 else (1.0, 0.5, 1.0)

        def cells_part(*refs, scales=scales):
            cells_kernel(scales[0], *refs)

        def owned_part(*refs, scales=scales):
            owned_kernel(scales, *refs)

        products, ghosts = call(
            cells_part,
            [shape(wide * slots + 8, LANES), shape(wide * face_rows, LANES)],
            [ANY] * 2 + [SMEM] + [VMEM] * 6,
            [
                pltpu.VMEM((wide * rows, LANES), jnp.float32),
                pltpu.VMEM((wide * points, LANES), jnp.float32),
                pltpu.VMEM((wide * points, LANES), jnp.float32),
                *[index] * 4,
                *[table] * 4,
                scratch,
                pltpu.SemaphoreType.DMA((9,)),
            ],
            mib=CELLS_MIB,
            cost=pl.CostEstimate(flops=2 * 10**9, bytes_accessed=10**7, transcendentals=0),
        )(doubled, pairs[chunks:], extra, current, *received, hamiltonian)
        partial = call(
            owned_part,
            shape(wide * nodes, LANES),
            [ANY] * 2 + [SMEM] + [VMEM] * 3,
            [*[table] * 4, scratch, pltpu.SemaphoreType.DMA((5,))],
            mib=2,
            cost=pl.CostEstimate(flops=10**9, bytes_accessed=10**7, transcendentals=0),
        )(doubled, pairs[:chunks], extra, products, current, previous)
        back = sent_ghosts(ghosts)
        if number < 3:
            previous = current
            current, face_vals = call(
                faces_kernel,
                [shape(wide * nodes, LANES), shape(wide * face_rows, LANES, jnp.bfloat16)],
                [SMEM] + [VMEM] * 5,
                [pltpu.VMEM((wide * face_rows, LANES), jnp.float32)],
                input_output_aliases={1: 0},
            )(faces, partial, *back)
            received = sent_faces(face_vals)
        else:
            half = shape(nodes // 2, columns, jnp.bfloat16)
            exact, mine, theirs, _ = call(
                last_kernel,
                [shape(nodes, columns), half, half, shape(wide * nodes, LANES)],
                [SMEM] + [VMEM] * 5,
                input_output_aliases={1: 3},
            )(faces, partial, *back)
    return finish(exact, mine, theirs)[None, None]


def dot_nodes(left, right):
    return lax.dot_general(left, right, (((0,), (0,)), ((), ())), preferred_element_type=jnp.float32)


def finish(exact, mine, theirs):
    nodes, columns = exact.shape
    domains = lax.axis_size(("dx", "dy"))
    near = passed_along(theirs, "band", 1)
    whole = dot_nodes(mine, mine) + dot_nodes(theirs, theirs)
    cross = dot_nodes(mine, near)
    far = passed_along(mine, "band", 1)
    pieces = jnp.concatenate(
        [whole[:, :LANES], whole[:, LANES:], cross[:, :LANES], cross[:, LANES:]], axis=0
    ).astype(jnp.bfloat16)
    pieces = pieces.reshape(domains, -1, LANES)
    pieces = lax.all_to_all(pieces, ("dx", "dy"), 0, 0, tiled=True)
    scale = 1.0 / (nodes * domains)

    def kernel(*refs):
        sum_kernel(scale, *refs)

    devices = lax.axis_size(("band", "dx", "dy"))
    sums = call(kernel, jax.ShapeDtypeStruct((devices, *pieces.shape[1:]), jnp.bfloat16), [VMEM], mib=4)(pieces)
    sums = lax.all_to_all(sums, ("band", "dx", "dy"), 0, 0, tiled=True)
    blocks = sums.reshape(2, -1, LANES)
    return call(
        rotate_kernel,
        shape(nodes, columns),
        [VMEM] * 4,
        [
            pltpu.VMEM((2 * columns, columns), jnp.float32),
            pltpu.VMEM((nodes, columns), jnp.float32),
            pltpu.SemaphoreType.DMA((nodes // 512,)),
        ],
        mib=14,
        out_specs=ANY,
    )(blocks, exact, near, far)


def solution(mesh):
    in_specs = (
        P("dx", "dy", None, "band"),
        P("dx", "dy", None, None, None),
        P("dx", "dy", None, None),
        P("dx", "dy", None, None),
    )
    out_specs = P("dx", "dy", None, "band")
    return jax.shard_map(local, mesh=mesh, in_specs=in_specs, out_specs=out_specs, check_vma=False)
```
